1024 devices in a mesh: gy: 64 (over y, z), gz: 16 (over x, core).
Axes of the slice: x: 8, y: 8, z: 8, core: 2. Of those that a mesh axis runs over, the one named last changes fastest.
Arguments:
- velocity: float32 [3, 2, 4096, 4096], P(None, None, 'gy', 'gz'), may hold values from -6 to 6
Outputs:
- deriv_y: float32 [3, 2, 4096, 4096], P(None, None, 'gy', 'gz')
- deriv_z: float32 [3, 2, 4096, 4096], P(None, None, 'gy', 'gz')
The draws below stay inside these ranges and needn't reach their ends.
All inputs are finite; a program needn't handle non-finite values.
Results may differ from the reference program's by a relative error of at most 0.00007.
Values sent between devices are 32-bit elements; how exact they have to be, the bound alone decides.
No kernel may reach another device: no remote copies, remote signals or barrier semaphores. Data moves between devices by JAX's collectives and lax.ppermute only.
A program may use at most 32 MiB of HBM per device.

```python
import math
import jax
import jax.numpy as jnp
from jax import lax

XW = 2
NY = 4096
NZ = 4096


def steps_of(stream_key, shape, cuts, low, top_value):
    def one(dim, blocks):
        steps = jax.random.uniform(jax.random.fold_in(jax.random.fold_in(stream_key, 6), dim), (blocks,), jnp.float32, low / len(cuts), top_value / len(cuts))
        return jnp.repeat(jnp.exp(steps), shape[dim] // blocks).reshape((-1,) + (1,) * (len(shape) - dim - 1))

    loudness = one(*cuts[0])
    for cut in cuts[1:]:
        loudness = loudness * one(*cut)
    return loudness


def normal_values(key, shape, scale, limit, cuts=(), kind=jnp.bfloat16):
    array = scale * jax.random.normal(key, shape, jnp.float32)
    if cuts:
        array = array * steps_of(key, shape, cuts, -0.22, 0.18)
    return jnp.clip(array, -limit, limit).astype(kind)


def setup_inputs(seed: int = 0) -> dict:
    arg_keys = jax.random.split(jax.random.key(seed), 2)
    velocity = normal_values(arg_keys[0], (3, XW, NY, NZ), 1.0, 6.0, ((2, 64), (3, 16)), jnp.float32)
    return {"velocity": velocity}


def derive(plane, axis):
    count = plane.shape[axis]
    spectrum = jnp.fft.rfft(plane, axis=axis)
    wave = 2.0 * math.pi * jnp.arange(count // 2 + 1, dtype=plane.dtype) / count
    factor = (14.0 / 9.0 * jnp.sin(wave) + jnp.sin(2.0 * wave) / 18.0) / (1.0 + 2.0 / 3.0 * jnp.cos(wave))
    if axis == 0:
        factor = factor[:, None]
    result = jnp.fft.irfft(spectrum * (1j * factor), n=count, axis=axis)
    return result.astype(plane.dtype)


def reference(velocity):
    planes = velocity.reshape(3 * XW, NY, NZ)

    def single(plane):
        return derive(plane, 0), derive(plane, 1)

    along_y, along_z = lax.map(single, planes)
    return along_y.reshape(velocity.shape), along_z.reshape(velocity.shape)
```

```python
import math

import jax
import jax.numpy as jnp
import numpy as np
from jax import lax
from jax.sharding import PartitionSpec as P

best = lax.Precision.HIGHEST


def response(lags):
    root = 1.5 - math.sqrt(5.0) / 2.0
    scale = root * 3.0 / (1.0 - root * root)

    def green(n):
        n = np.abs(n)
        return scale * np.where(n % 2 == 0, 1.0, -1.0) * root ** n.astype(np.float64)

    n = np.asarray(lags)
    near = 7.0 / 9.0 * (green(n + 1) - green(n - 1))
    far = 1.0 / 36.0 * (green(n + 2) - green(n - 2))
    return near + far


def operator(rows, cols):
    return response(np.asarray(rows)[:, None] - np.asarray(cols)[None, :])


def tails(count):
    root = 1.5 - math.sqrt(5.0) / 2.0
    cells = np.arange(count)
    low = np.zeros((count, 2))
    low[0, 0] = 1.0
    low[1:, 1] = (-root) ** (cells[1:] - 1.0)
    return low, low[::-1, ::-1]


def f32(array):
    return jnp.asarray(np.asarray(array, np.float32))


def shifted(shard, axis, by):
    count = lax.axis_size(axis)
    return lax.ppermute(shard, axis, [(i, (i + by) % count) for i in range(count)])


def per_device(velocity):
    shape = velocity.shape
    ny, nz = shape[2], shape[3]
    u = velocity.reshape(shape[0] * shape[1], ny, nz)
    lines = u.reshape(-1, nz)
    cells_y, cells_z = np.arange(ny), np.arange(nz)

    up_y = jnp.einsum("kj,pjz->pkz", f32(operator([ny, ny + 1], cells_y)), u, precision=best)
    down_y = jnp.einsum("kj,pjz->pkz", f32(operator([-2, -1], cells_y)), u, precision=best)
    up_z = jnp.einsum("kj,lj->kl", f32(operator([nz, nz + 1], cells_z)), lines, precision=best)
    down_z = jnp.einsum("kj,lj->kl", f32(operator([-2, -1], cells_z)), lines, precision=best)

    low_y = shifted(up_y, "gy", 1)
    high_y = shifted(down_y, "gy", -1)
    low_z = shifted(up_z, "gz", 1)
    high_z = shifted(down_z, "gz", -1)

    local_y = jnp.einsum("ij,pjz->piz", f32(operator(cells_y, cells_y)), u, precision=best)
    local_z = jnp.einsum("lj,ij->li", lines, f32(operator(cells_z, cells_z)), precision=best)

    spread_low_y, spread_high_y = tails(ny)
    spread_low_z, spread_high_z = tails(nz)
    deriv_y = local_y + jnp.einsum("ik,pkz->piz", f32(spread_low_y), low_y, precision=best)
    deriv_y = deriv_y + jnp.einsum("ik,pkz->piz", f32(spread_high_y), high_y, precision=best)
    deriv_z = local_z + jnp.einsum("kl,ik->li", low_z, f32(spread_low_z), precision=best)
    deriv_z = deriv_z + jnp.einsum("kl,ik->li", high_z, f32(spread_high_z), precision=best)
    return deriv_y.reshape(shape), deriv_z.reshape(shape)


def solution(mesh):
    in_specs = (P(None, None, "gy", "gz"),)
    out_specs = (P(None, None, "gy", "gz"), P(None, None, "gy", "gz"))
    return jax.shard_map(
        per_device, mesh=mesh, in_specs=in_specs, out_specs=out_specs, check_vma=False
    )
```

```python
import math

import jax
import jax.numpy as jnp
import numpy as np
from jax import lax
from jax.experimental import pallas as pl
from jax.experimental.pallas import tpu as pltpu
from jax.sharding import PartitionSpec as P

best = lax.Precision.HIGHEST
vmem = 4 << 20
root = 1.5 - math.sqrt(5.0) / 2.0
log_root = math.log2(root)


def response(n):
    scale = root * 3.0 / (1.0 - root * root)

    def green(n):
        return scale * (-1.0) ** abs(n) * root ** abs(n)

    return 7.0 / 9.0 * (green(n + 1) - green(n - 1)) + 1.0 / 36.0 * (green(n + 2) - green(n - 2))


far_scale = response(2) / root**2
near_extra = response(1) + far_scale * root


def decay(n):
    return jnp.where(n % 2 == 0, 1.0, -1.0) * jnp.exp2(n.astype(jnp.float32) * log_root)


def operator(shape, row_start, row_dim):
    lag = row_start + lax.broadcasted_iota(jnp.int32, shape, row_dim) - lax.broadcasted_iota(jnp.int32, shape, 1 - row_dim)
    size = jnp.abs(lag)
    weight = far_scale * decay(size) + jnp.where(size == 1, near_extra, 0.0)
    return jnp.where(lag == 0, 0.0, jnp.where(lag > 0, weight, -weight))


def edges_kernel(u_hbm, up_ref, down_ref, u_ref, sem):
    planes, ny, nz = u_ref.shape
    copies = [pltpu.make_async_copy(u_hbm.at[p], u_ref.at[p], sem.at[p]) for p in range(planes)]
    for copy in copies:
        copy.start()
    row = lax.broadcasted_iota(jnp.int32, (ny, nz), 0)
    up_weight = far_scale * decay(ny + 1 - row)
    down_weight = -far_scale * decay(row + 2)
    for p in range(planes):
        copies[p].wait()
        u = u_ref[p]
        up = jnp.sum(u * up_weight, axis=0, keepdims=True)
        down = jnp.sum(u * down_weight, axis=0, keepdims=True)
        up_ref[p, 0:1, :] = up * (-1.0 / root) + near_extra * u[ny - 1 : ny]
        up_ref[p, 1:2, :] = up
        down_ref[p, 0:1, :] = down
        down_ref[p, 1:2, :] = down * (-1.0 / root) - near_extra * u[0:1]


def edges(u):
    planes, ny, nz = u.shape
    out = jax.ShapeDtypeStruct((planes, 2, nz), jnp.float32)
    return pl.pallas_call(
        edges_kernel,
        out_shape=(out, out),
        in_specs=[pl.BlockSpec(memory_space=pl.ANY)],
        out_specs=(pl.BlockSpec(memory_space=pltpu.VMEM), pl.BlockSpec(memory_space=pltpu.VMEM)),
        scratch_shapes=[pltpu.VMEM(u.shape, jnp.float32), pltpu.SemaphoreType.DMA((planes,))],
        compiler_params=pltpu.CompilerParams(vmem_limit_bytes=vmem),
        name="edges_y",
    )(u)


def join_kernel(local_ref, low_ref, high_ref, out_hbm, out_ref, sem):
    planes, ny, nz = local_ref.shape
    row = lax.broadcasted_iota(jnp.int32, (ny, nz), 0)
    low_decay = decay(jnp.maximum(row - 1, 0))
    high_decay = decay(jnp.maximum(ny - 2 - row, 0))
    copies = []
    for p in range(planes):
        low = jnp.where(row == 0, low_ref[p, 0:1, :], low_ref[p, 1:2, :] * low_decay)
        high = jnp.where(row == ny - 1, high_ref[p, 1:2, :], high_ref[p, 0:1, :] * high_decay)
        out_ref[p] = local_ref[p] + low + high
        copies.append(pltpu.make_async_copy(out_ref.at[p], out_hbm.at[p], sem.at[p]))
        copies[p].start()
    for copy in copies:
        copy.wait()


def join(local, low, high):
    planes = local.shape[0]
    return pl.pallas_call(
        join_kernel,
        out_shape=jax.ShapeDtypeStruct(local.shape, jnp.float32),
        in_specs=[pl.BlockSpec(memory_space=pltpu.VMEM)] * 3,
        out_specs=pl.BlockSpec(memory_space=pl.ANY),
        scratch_shapes=[pltpu.VMEM(local.shape, jnp.float32), pltpu.SemaphoreType.DMA((planes,))],
        compiler_params=pltpu.CompilerParams(vmem_limit_bytes=vmem),
        name="join_y",
    )(local, low, high)


def local_kernel(u_ref, z_ref, y_ref):
    planes, ny, nz = u_ref.shape
    along = operator((nz, nz), 0, 1)
    across = operator((ny, ny), 0, 0)
    for p in range(planes):
        z_ref[p] = jnp.dot(u_ref[p], along, precision=best, preferred_element_type=jnp.float32)
        y_ref[p] = jnp.dot(across, u_ref[p], precision=best, preferred_element_type=jnp.float32)


def local_parts(u):
    out = jax.ShapeDtypeStruct(u.shape, jnp.float32)
    here = pl.BlockSpec(memory_space=pltpu.VMEM)
    return pl.pallas_call(
        local_kernel,
        out_shape=(out, out),
        in_specs=[here],
        out_specs=(here, here),
        compiler_params=pltpu.CompilerParams(vmem_limit_bytes=vmem),
        cost_estimate=pl.CostEstimate(flops=2 * u.size * 512, bytes_accessed=12 * u.size, transcendentals=70000),
        name="local_parts",
    )(u)


def join_z_kernel(local_ref, low_ref, high_ref, out_hbm, out_ref, sem):
    planes, ny, nz = local_ref.shape
    ends = jnp.concatenate([low_ref[...], high_ref[...], low_ref[...], high_ref[...]], axis=0)
    ends = jnp.transpose(ends)
    cell = lax.broadcasted_iota(jnp.int32, (1, nz), 1)
    low_first = jnp.where(cell == 0, 1.0, 0.0)
    low_rest = jnp.where(cell == 0, 0.0, decay(jnp.maximum(cell - 1, 0)))
    high_first = jnp.where(cell == nz - 1, 1.0, 0.0)
    high_rest = jnp.where(cell == nz - 1, 0.0, decay(jnp.maximum(nz - 2 - cell, 0)))
    copies = []
    for p in range(planes):
        end = ends[p * ny : (p + 1) * ny]
        low = end[:, 0:1] * low_first + end[:, 1:2] * low_rest
        high = end[:, 2:3] * high_rest + end[:, 3:4] * high_first
        out_ref[p] = local_ref[p] + low + high
        copies.append(pltpu.make_async_copy(out_ref.at[p], out_hbm.at[p], sem.at[p]))
        copies[p].start()
    for copy in copies:
        copy.wait()


def join_z(local, low, high):
    planes = local.shape[0]
    return pl.pallas_call(
        join_z_kernel,
        out_shape=jax.ShapeDtypeStruct(local.shape, jnp.float32),
        in_specs=[pl.BlockSpec(memory_space=pltpu.VMEM)] * 3,
        out_specs=pl.BlockSpec(memory_space=pl.ANY),
        scratch_shapes=[pltpu.VMEM(local.shape, jnp.float32), pltpu.SemaphoreType.DMA((planes,))],
        compiler_params=pltpu.CompilerParams(vmem_limit_bytes=vmem),
        name="join_z",
    )(local, low, high)


def place_kernel(u_hbm, out_hbm):
    pass


def place(u):
    return pl.pallas_call(
        place_kernel,
        out_shape=jax.ShapeDtypeStruct(u.shape, u.dtype),
        in_specs=[pl.BlockSpec(memory_space=pl.ANY)],
        out_specs=pl.BlockSpec(memory_space=pl.ANY),
        compiler_params=pltpu.CompilerParams(vmem_limit_bytes=vmem),
        name="place_z",
    )(u)


def shifted(shard, axis, by):
    count = lax.axis_size(axis)
    return lax.ppermute(shard, axis, [(i, (i + by) % count) for i in range(count)])


def along_z(u):
    nz = u.shape[2]
    lines = u.reshape(-1, nz)
    up = jnp.einsum("kj,lj->kl", operator((2, nz), nz, 0), lines, precision=best)
    down = jnp.einsum("kj,lj->kl", operator((2, nz), -2, 0), lines, precision=best)
    low = shifted(up, "gz", 1)
    high = shifted(down, "gz", -1)
    local_z, local_y = local_parts(u)
    return join_z(local_z, low, high), local_y


def per_device(velocity):
    shape = velocity.shape
    u = velocity.reshape(shape[0] * shape[1], shape[2], shape[3])
    late = lax.axis_index("gy") % 8 == 7
    up_y, down_y = edges(u)
    low_y = shifted(up_y, "gy", 1)
    deriv_z, local_y = lax.cond(
        late, lambda u: (place(u), jnp.zeros_like(u)), along_z, u
    )
    down_y, deriv_z, local_y = lax.optimization_barrier((down_y, deriv_z, local_y))
    high_y = shifted(down_y, "gy", -1)
    deriv_z, local_y = lax.cond(late, lambda u, z, y: along_z(u), lambda u, z, y: (z, y), u, deriv_z, local_y)
    deriv_y = join(local_y, low_y, high_y)
    return deriv_y.reshape(shape), deriv_z.reshape(shape)


def solution(mesh):
    in_specs = (P(None, None, "gy", "gz"),)
    out_specs = (P(None, None, "gy", "gz"), P(None, None, "gy", "gz"))
    return jax.shard_map(
        per_device, mesh=mesh, in_specs=in_specs, out_specs=out_specs, check_vma=False
    )
```

```python
import math

import jax
import jax.numpy as jnp
import numpy as np
from jax import lax
from jax.experimental import pallas as pl
from jax.experimental.pallas import tpu as pltpu
from jax.sharding import PartitionSpec as P

best = lax.Precision.HIGHEST
vmem = 4 << 20
column = 8
root = 1.5 - math.sqrt(5.0) / 2.0
log_root = math.log2(root)


def response(n):
    scale = root * 3.0 / (1.0 - root * root)

    def green(n):
        return scale * (-1.0) ** abs(n) * root ** abs(n)

    return 7.0 / 9.0 * (green(n + 1) - green(n - 1)) + 1.0 / 36.0 * (green(n + 2) - green(n - 2))


far_scale = response(2) / root**2
near_extra = response(1) + far_scale * root


def decay(n):
    return jnp.where(n % 2 == 0, 1.0, -1.0) * jnp.exp2(n.astype(jnp.float32) * log_root)


def operator(shape, row_start, row_dim):
    lag = row_start + lax.broadcasted_iota(jnp.int32, shape, row_dim) - lax.broadcasted_iota(jnp.int32, shape, 1 - row_dim)
    size = jnp.abs(lag)
    weight = far_scale * decay(size) + jnp.where(size == 1, near_extra, 0.0)
    return jnp.where(lag == 0, 0.0, jnp.where(lag > 0, weight, -weight))


def edges_kernel(u_hbm, up_ref, down_ref, up_in_ref, down_in_ref, pair_ref, u_ref, sem):
    planes, ny, nz = u_ref.shape
    even = lax.axis_index("gy") % 2 == 0
    copies = [pltpu.make_async_copy(u_hbm.at[p], u_ref.at[p], sem.at[p]) for p in range(planes)]
    for copy in copies:
        copy.start()
    row = lax.broadcasted_iota(jnp.int32, (ny, nz), 0)
    up_weight = far_scale * decay(ny + 1 - row)
    down_weight = -far_scale * decay(row + 2)
    for p in range(planes):
        copies[p].wait()
        u = u_ref[p]
        up = jnp.sum(u * up_weight, axis=0, keepdims=True)
        down = jnp.sum(u * down_weight, axis=0, keepdims=True)
        up_near = up * (-1.0 / root) + near_extra * u[ny - 1 : ny]
        down_near = down * (-1.0 / root) - near_extra * u[0:1]
        for ref in (up_ref, up_in_ref):
            ref[p, 0:1, :] = up_near
            ref[p, 1:2, :] = up
        for ref in (down_ref, down_in_ref):
            ref[p, 0:1, :] = down
            ref[p, 1:2, :] = down_near
        pair_ref[p, 0:1, :] = jnp.where(even, up_near, down)
        pair_ref[p, 1:2, :] = jnp.where(even, up, down_near)


def edges(u):
    planes, ny, nz = u.shape
    out = pltpu.VMEM((planes, 2, nz), jnp.float32)
    return pl.pallas_call(
        edges_kernel,
        out_shape=(out,) * 5,
        in_specs=[pl.BlockSpec(memory_space=pl.ANY)],
        out_specs=(pl.BlockSpec(memory_space=pltpu.VMEM),) * 5,
        scratch_shapes=[pltpu.VMEM(u.shape, jnp.float32), pltpu.SemaphoreType.DMA((planes,))],
        compiler_params=pltpu.CompilerParams(vmem_limit_bytes=vmem),
        name="edges_y",
    )(u)


def join_rows(local_ref, low_of, high_of, out_hbm, out_ref, sem):
    planes, ny, nz = local_ref.shape
    row = lax.broadcasted_iota(jnp.int32, (ny, nz), 0)
    low_decay = decay(jnp.maximum(row - 1, 0))
    high_decay = decay(jnp.maximum(ny - 2 - row, 0))
    copies = []
    for p in range(planes):
        low, high = low_of(p), high_of(p)
        low = jnp.where(row == 0, low[0:1], low[1:2] * low_decay)
        high = jnp.where(row == ny - 1, high[1:2], high[0:1] * high_decay)
        out_ref[p] = local_ref[p] + low + high
        copies.append(pltpu.make_async_copy(out_ref.at[p], out_hbm.at[p], sem.at[p]))
        copies[p].start()
    for copy in copies:
        copy.wait()


def join_kernel(local_ref, wrap_ref, low_ref, high_ref, out_hbm, out_ref, sem):
    place = lax.axis_index("gy") % column

    @pl.when(place != column - 1)
    def _():
        def low(p):
            return jnp.where(place == 0, wrap_ref[p], low_ref[p])

        join_rows(local_ref, low, lambda p: high_ref[p], out_hbm, out_ref, sem)


def join_last_kernel(made_hbm, local_ref, low_ref, wrap_ref, out_hbm, out_ref, sem):
    @pl.when(lax.axis_index("gy") % column == column - 1)
    def _():
        join_rows(local_ref, lambda p: low_ref[p], lambda p: wrap_ref[p], out_hbm, out_ref, sem)


def join(local, *ends):
    planes = local.shape[0]
    return pl.pallas_call(
        join_kernel,
        out_shape=jax.ShapeDtypeStruct(local.shape, jnp.float32),
        in_specs=[pl.BlockSpec(memory_space=pltpu.VMEM)] * 4,
        out_specs=pl.BlockSpec(memory_space=pl.ANY),
        scratch_shapes=[pltpu.VMEM(local.shape, jnp.float32), pltpu.SemaphoreType.DMA((planes,))],
        compiler_params=pltpu.CompilerParams(vmem_limit_bytes=vmem),
        cost_estimate=pl.CostEstimate(flops=6 * local.size, bytes_accessed=8 * local.size, transcendentals=32768),
        name="join_y",
    )(*(pltpu.with_memory_space_constraint(end, pltpu.VMEM) for end in (local, *ends)))


def join_last(made, local, low, wrap):
    planes = local.shape[0]
    return pl.pallas_call(
        join_last_kernel,
        out_shape=jax.ShapeDtypeStruct(local.shape, jnp.float32),
        in_specs=[pl.BlockSpec(memory_space=pl.ANY)] + [pl.BlockSpec(memory_space=pltpu.VMEM)] * 3,
        out_specs=pl.BlockSpec(memory_space=pl.ANY),
        scratch_shapes=[pltpu.VMEM(local.shape, jnp.float32), pltpu.SemaphoreType.DMA((planes,))],
        compiler_params=pltpu.CompilerParams(vmem_limit_bytes=vmem),
        input_output_aliases={0: 0},
        name="join_y_last",
    )(made, *(pltpu.with_memory_space_constraint(end, pltpu.VMEM) for end in (local, low, wrap)))


def edges_z_kernel(u_ref, up_ref, down_ref):
    planes, ny, nz = u_ref.shape
    which = lax.broadcasted_iota(jnp.int32, (8, nz), 0)
    cell = lax.broadcasted_iota(jnp.int32, (8, nz), 1)
    target = jnp.where(which < 2, nz + which, which - 4)
    lag = target - cell
    size = jnp.abs(lag)
    weight = far_scale * decay(size) + jnp.where(size == 1, near_extra, 0.0)
    weight = jnp.where(lag > 0, weight, -weight)
    ends = lax.dot_general(
        weight, u_ref[...].reshape(planes * ny, nz), (((1,), (1,)), ((), ())), precision=best, preferred_element_type=jnp.float32
    )
    up_ref[...] = ends[0:2]
    down_ref[...] = ends[2:4]


def edges_z(u):
    out = jax.ShapeDtypeStruct((2, u.shape[0] * u.shape[1]), jnp.float32)
    here = pl.BlockSpec(memory_space=pltpu.VMEM)
    return pl.pallas_call(
        edges_z_kernel,
        out_shape=(out, out),
        in_specs=[here],
        out_specs=(here, here),
        compiler_params=pltpu.CompilerParams(vmem_limit_bytes=vmem),
        name="edges_z",
    )(u)


def local_kernel(u_ref, z_ref, y_ref):
    planes, ny, nz = u_ref.shape
    along = operator((nz, nz), 0, 1)
    across = operator((ny, ny), 0, 0)
    for p in range(planes):
        z_ref[p] = jnp.dot(u_ref[p], along, precision=best, preferred_element_type=jnp.float32)
        y_ref[p] = jnp.dot(across, u_ref[p], precision=best, preferred_element_type=jnp.float32)


def local_parts(u):
    out = jax.ShapeDtypeStruct(u.shape, jnp.float32)
    here = pl.BlockSpec(memory_space=pltpu.VMEM)
    return pl.pallas_call(
        local_kernel,
        out_shape=(out, out),
        in_specs=[here],
        out_specs=(here, here),
        compiler_params=pltpu.CompilerParams(vmem_limit_bytes=vmem),
        cost_estimate=pl.CostEstimate(flops=2 * u.size * 512, bytes_accessed=12 * u.size, transcendentals=70000),
        name="local_parts",
    )(u)


def join_z_kernel(local_ref, high_ref, low_ref, out_hbm, out_ref, sem):
    planes, ny, nz = local_ref.shape
    ends = jnp.concatenate([low_ref[...], high_ref[...], low_ref[...], high_ref[...]], axis=0)
    ends = jnp.transpose(ends)
    cell = lax.broadcasted_iota(jnp.int32, (1, nz), 1)
    low_first = jnp.where(cell == 0, 1.0, 0.0)
    low_rest = jnp.where(cell == 0, 0.0, decay(jnp.maximum(cell - 1, 0)))
    high_first = jnp.where(cell == nz - 1, 1.0, 0.0)
    high_rest = jnp.where(cell == nz - 1, 0.0, decay(jnp.maximum(nz - 2 - cell, 0)))
    copies = []
    for p in range(planes):
        end = ends[p * ny : (p + 1) * ny]
        low = end[:, 0:1] * low_first + end[:, 1:2] * low_rest
        high = end[:, 2:3] * high_rest + end[:, 3:4] * high_first
        out_ref[p] = local_ref[p] + low + high
        copies.append(pltpu.make_async_copy(out_ref.at[p], out_hbm.at[p], sem.at[p]))
        copies[p].start()
    for copy in copies:
        copy.wait()


def join_z(local, low, high):
    planes = local.shape[0]
    return pl.pallas_call(
        join_z_kernel,
        out_shape=jax.ShapeDtypeStruct(local.shape, jnp.float32),
        in_specs=[pl.BlockSpec(memory_space=pltpu.VMEM)] * 3,
        out_specs=pl.BlockSpec(memory_space=pl.ANY),
        scratch_shapes=[pltpu.VMEM(local.shape, jnp.float32), pltpu.SemaphoreType.DMA((planes,))],
        compiler_params=pltpu.CompilerParams(vmem_limit_bytes=vmem),
        name="join_z",
    )(local, high, low)


def place_kernel(u_hbm, out_hbm):
    pass


def place_z(u):
    return pl.pallas_call(
        place_kernel,
        out_shape=jax.ShapeDtypeStruct(u.shape, u.dtype),
        in_specs=[pl.BlockSpec(memory_space=pl.ANY)],
        out_specs=pl.BlockSpec(memory_space=pl.ANY),
        compiler_params=pltpu.CompilerParams(vmem_limit_bytes=vmem),
        name="place_z",
    )(u)


def shifted(shard, axis, by):
    count = lax.axis_size(axis)
    return lax.ppermute(shard, axis, [(i, (i + by) % count) for i in range(count)])


def linked(shard, pairs):
    return lax.ppermute(shard, "gy", pairs)


def along_z(u, pair=None, links=None):
    up, down = edges_z(u)
    high = shifted(down, "gz", -1)
    low = shifted(up, "gz", 1)
    local_z, local_y = local_parts(u)
    if links is None:
        return join_z(local_z, low, high), local_y
    high, low, pair = lax.optimization_barrier((high, low, pair))
    there = lax.ppermute(pair, ("gy", "gz"), links)
    return join_z(local_z, low, high), local_y, there


def per_device(velocity):
    shape = velocity.shape
    u = velocity.reshape(shape[0] * shape[1], shape[2], shape[3])
    count, width = lax.axis_size("gy"), lax.axis_size("gz")
    row, place = lax.axis_index("gy"), lax.axis_index("gy") % column
    slow = (lax.axis_index("gz") == 0) & (row < 2)
    ends = range(count)
    final = [(i, i ^ 1) for i in ends if i % column >= column - 2]
    inner = [(i, i + 1) for i in ends if 1 <= i % column < column - 2]
    wrap = [(i, (i + 1) % count) for i in ends if i % column == column - 1]
    last = [(0, width), (width, 0)]
    first = [(i * width + k, (i ^ 1) * width + k) for i in ends if i % column < 2 for k in range(width)]
    first = [link for link in first if link not in last]

    def back(pairs):
        return [(b, a) for a, b in pairs]

    def early(u, up, down, pair):
        pair_in = lax.ppermute(pair, ("gy", "gz"), first)
        low = linked(up, inner)
        high = linked(down, back(inner))
        u, pair_in = lax.optimization_barrier((u, pair_in))
        deriv_z, local_y, there = along_z(u, pair, last)
        pair_in = jnp.where(slow, there, pair_in)
        return deriv_z, local_y, jnp.where(place == 1, pair_in, low), jnp.where(place == 0, pair_in, high)

    def skip(u, up, down, pair):
        return place_z(u), jnp.zeros_like(u), jnp.zeros_like(up), jnp.zeros_like(down)

    up, down, up_in, down_in, pair = edges(u)
    low_wrap = linked(up, wrap)
    deriv_z, local_y, low, high = lax.cond(place == column - 1, skip, early, u, up_in, down_in, pair)
    down, deriv_z, local_y, low, high = lax.optimization_barrier((down, deriv_z, local_y, low, high))
    high_wrap = linked(down, back(wrap))
    deriv_z, local_y = lax.cond(place == column - 1, lambda u, z, y: along_z(u), lambda u, z, y: (z, y), u, deriv_z, local_y)
    pair, high, deriv_z, local_y = lax.optimization_barrier((pair, high, deriv_z, local_y))
    high = lax.cond(place >= column - 2, lambda pair, high: linked(pair, final), lambda pair, high: high, pair, high)
    deriv_y = join(local_y, low_wrap, low, high)
    deriv_y = join_last(deriv_y, local_y, high, high_wrap)
    return deriv_y.reshape(shape), deriv_z.reshape(shape)


def solution(mesh):
    in_specs = (P(None, None, "gy", "gz"),)
    out_specs = (P(None, None, "gy", "gz"), P(None, None, "gy", "gz"))
    return jax.shard_map(
        per_device, mesh=mesh, in_specs=in_specs, out_specs=out_specs, check_vma=False
    )
```

```python
import math

import jax
import jax.numpy as jnp
import numpy as np
from jax import lax
from jax.experimental import pallas as pl
from jax.experimental.pallas import tpu as pltpu
from jax.sharding import PartitionSpec as P

best = lax.Precision.HIGHEST
vmem = 4 << 20
column = 8
root = 1.5 - math.sqrt(5.0) / 2.0
log_root = math.log2(root)


def response(n):
    scale = root * 3.0 / (1.0 - root * root)

    def green(n):
        return scale * (-1.0) ** abs(n) * root ** abs(n)

    return 7.0 / 9.0 * (green(n + 1) - green(n - 1)) + 1.0 / 36.0 * (green(n + 2) - green(n - 2))


far_scale = response(2) / root**2
near_extra = response(1) + far_scale * root


def decay(n):
    return jnp.where(n % 2 == 0, 1.0, -1.0) * jnp.exp2(n.astype(jnp.float32) * log_root)


def operator(shape, row_start, row_dim):
    lag = row_start + lax.broadcasted_iota(jnp.int32, shape, row_dim) - lax.broadcasted_iota(jnp.int32, shape, 1 - row_dim)
    size = jnp.abs(lag)
    weight = far_scale * decay(size) + jnp.where(size == 1, near_extra, 0.0)
    return jnp.where(lag == 0, 0.0, jnp.where(lag > 0, weight, -weight))


def edges_kernel(u_hbm, u_ref, up_ref, down_ref, up_in_ref, down_in_ref, pair_ref, sem):
    planes, ny, nz = u_ref.shape
    even = lax.axis_index("gy") % 2 == 0
    copies = [pltpu.make_async_copy(u_hbm.at[p], u_ref.at[p], sem.at[p]) for p in range(planes)]
    for copy in copies:
        copy.start()
    row = lax.broadcasted_iota(jnp.int32, (ny, nz), 0)
    up_weight = far_scale * decay(ny + 1 - row)
    down_weight = -far_scale * decay(row + 2)
    for p in range(planes):
        copies[p].wait()
        u = u_ref[p]
        up = jnp.sum(u * up_weight, axis=0, keepdims=True)
        down = jnp.sum(u * down_weight, axis=0, keepdims=True)
        up_near = up * (-1.0 / root) + near_extra * u[ny - 1 : ny]
        down_near = down * (-1.0 / root) - near_extra * u[0:1]
        for ref in (up_ref, up_in_ref):
            ref[p, 0:1, :] = up_near
            ref[p, 1:2, :] = up
        for ref in (down_ref, down_in_ref):
            ref[p, 0:1, :] = down
            ref[p, 1:2, :] = down_near
        pair_ref[p, 0:1, :] = jnp.where(even, up_near, down)
        pair_ref[p, 1:2, :] = jnp.where(even, up, down_near)


def edges(u):
    planes, ny, nz = u.shape
    out = pltpu.VMEM((planes, 2, nz), jnp.float32)
    return pl.pallas_call(
        edges_kernel,
        out_shape=(pltpu.VMEM(u.shape, jnp.float32),) + (out,) * 5,
        in_specs=[pl.BlockSpec(memory_space=pl.ANY)],
        out_specs=(pl.BlockSpec(memory_space=pltpu.VMEM),) * 6,
        scratch_shapes=[pltpu.SemaphoreType.DMA((planes,))],
        compiler_params=pltpu.CompilerParams(vmem_limit_bytes=vmem),
        name="edges_y",
    )(pltpu.with_memory_space_constraint(u, pltpu.HBM))


def join_rows(local_ref, low_of, high_of, out_hbm, out_ref, sem):
    planes, ny, nz = local_ref.shape
    row = lax.broadcasted_iota(jnp.int32, (ny, nz), 0)
    low_decay = decay(jnp.maximum(row - 1, 0))
    high_decay = decay(jnp.maximum(ny - 2 - row, 0))
    copies = []
    for p in range(planes):
        low, high = low_of(p), high_of(p)
        low = jnp.where(row == 0, low[0:1], low[1:2] * low_decay)
        high = jnp.where(row == ny - 1, high[1:2], high[0:1] * high_decay)
        out_ref[p] = local_ref[p] + low + high
        copies.append(pltpu.make_async_copy(out_ref.at[p], out_hbm.at[p], sem.at[p]))
        copies[p].start()
    for copy in copies:
        copy.wait()


def join_kernel(local_ref, wrap_ref, low_ref, high_ref, out_hbm, out_ref, sem):
    place = lax.axis_index("gy") % column

    @pl.when(place != column - 1)
    def _():
        def low(p):
            return jnp.where(place == 0, wrap_ref[p], low_ref[p])

        join_rows(local_ref, low, lambda p: high_ref[p], out_hbm, out_ref, sem)


def join_last_kernel(made_hbm, local_ref, low_ref, wrap_ref, out_hbm, out_ref, sem):
    @pl.when(lax.axis_index("gy") % column == column - 1)
    def _():
        join_rows(local_ref, lambda p: low_ref[p], lambda p: wrap_ref[p], out_hbm, out_ref, sem)


def join(local, *ends):
    planes = local.shape[0]
    return pl.pallas_call(
        join_kernel,
        out_shape=jax.ShapeDtypeStruct(local.shape, jnp.float32),
        in_specs=[pl.BlockSpec(memory_space=pltpu.VMEM)] * 4,
        out_specs=pl.BlockSpec(memory_space=pl.ANY),
        scratch_shapes=[pltpu.VMEM(local.shape, jnp.float32), pltpu.SemaphoreType.DMA((planes,))],
        compiler_params=pltpu.CompilerParams(vmem_limit_bytes=vmem),
        cost_estimate=pl.CostEstimate(flops=6 * local.size, bytes_accessed=8 * local.size, transcendentals=32768),
        name="join_y",
    )(*(pltpu.with_memory_space_constraint(end, pltpu.VMEM) for end in (local, *ends)))


def join_last(made, local, low, wrap):
    planes = local.shape[0]
    return pl.pallas_call(
        join_last_kernel,
        out_shape=jax.ShapeDtypeStruct(local.shape, jnp.float32),
        in_specs=[pl.BlockSpec(memory_space=pl.ANY)] + [pl.BlockSpec(memory_space=pltpu.VMEM)] * 3,
        out_specs=pl.BlockSpec(memory_space=pl.ANY),
        scratch_shapes=[pltpu.VMEM(local.shape, jnp.float32), pltpu.SemaphoreType.DMA((planes,))],
        compiler_params=pltpu.CompilerParams(vmem_limit_bytes=vmem),
        input_output_aliases={0: 0},
        name="join_y_last",
    )(made, *(pltpu.with_memory_space_constraint(end, pltpu.VMEM) for end in (local, low, wrap)))


def edges_z_kernel(u_ref, up_ref, down_ref):
    planes, ny, nz = u_ref.shape
    which = lax.broadcasted_iota(jnp.int32, (8, nz), 0)
    cell = lax.broadcasted_iota(jnp.int32, (8, nz), 1)
    target = jnp.where(which < 2, nz + which, which - 4)
    lag = target - cell
    size = jnp.abs(lag)
    weight = far_scale * decay(size) + jnp.where(size == 1, near_extra, 0.0)
    weight = jnp.where(lag > 0, weight, -weight)
    ends = lax.dot_general(
        weight, u_ref[...].reshape(planes * ny, nz), (((1,), (1,)), ((), ())), precision=best, preferred_element_type=jnp.float32
    )
    up_ref[...] = ends[0:2]
    down_ref[...] = ends[2:4]


def edges_z(u):
    out = jax.ShapeDtypeStruct((2, u.shape[0] * u.shape[1]), jnp.float32)
    here = pl.BlockSpec(memory_space=pltpu.VMEM)
    return pl.pallas_call(
        edges_z_kernel,
        out_shape=(out, out),
        in_specs=[here],
        out_specs=(here, here),
        compiler_params=pltpu.CompilerParams(vmem_limit_bytes=vmem),
        name="edges_z",
    )(u)


def local_kernel(u_ref, z_ref, y_ref):
    planes, ny, nz = u_ref.shape
    lines = u_ref[...].reshape(planes * ny, nz)
    across = operator((ny, ny), 0, 0)
    along_z = jnp.dot(lines, operator((nz, nz), 0, 1), precision=best, preferred_element_type=jnp.float32)
    z_ref[...] = along_z.reshape(planes, ny, nz)
    for p in range(planes):
        y_ref[p] = jnp.dot(across, u_ref[p], precision=best, preferred_element_type=jnp.float32)


def local_parts(u):
    out = jax.ShapeDtypeStruct(u.shape, jnp.float32)
    here = pl.BlockSpec(memory_space=pltpu.VMEM)
    return pl.pallas_call(
        local_kernel,
        out_shape=(out, out),
        in_specs=[here],
        out_specs=(here, here),
        compiler_params=pltpu.CompilerParams(vmem_limit_bytes=vmem),
        cost_estimate=pl.CostEstimate(flops=2 * u.size * 512, bytes_accessed=12 * u.size, transcendentals=70000),
        name="local_parts",
    )(u)


def join_z_kernel(local_ref, high_ref, low_ref, out_ref):
    planes, ny, nz = local_ref.shape
    ends = jnp.concatenate([low_ref[...], high_ref[...], low_ref[...], high_ref[...]], axis=0)
    ends = jnp.transpose(ends)
    cell = lax.broadcasted_iota(jnp.int32, (1, nz), 1)
    low_first = jnp.where(cell == 0, 1.0, 0.0)
    low_rest = jnp.where(cell == 0, 0.0, decay(jnp.maximum(cell - 1, 0)))
    high_first = jnp.where(cell == nz - 1, 1.0, 0.0)
    high_rest = jnp.where(cell == nz - 1, 0.0, decay(jnp.maximum(nz - 2 - cell, 0)))
    for p in range(planes):
        end = ends[p * ny : (p + 1) * ny]
        low = end[:, 0:1] * low_first + end[:, 1:2] * low_rest
        high = end[:, 2:3] * high_rest + end[:, 3:4] * high_first
        out_ref[p] = local_ref[p] + low + high


def join_z(local, low, high):
    here = pl.BlockSpec(memory_space=pltpu.VMEM)
    return pl.pallas_call(
        join_z_kernel,
        out_shape=jax.ShapeDtypeStruct(local.shape, jnp.float32),
        in_specs=[here] * 3,
        out_specs=here,
        compiler_params=pltpu.CompilerParams(vmem_limit_bytes=vmem),
        name="join_z",
    )(local, high, low)


def place_kernel(u_hbm, out_hbm):
    pass


def place_z(u):
    return pl.pallas_call(
        place_kernel,
        out_shape=jax.ShapeDtypeStruct(u.shape, u.dtype),
        in_specs=[pl.BlockSpec(memory_space=pl.ANY)],
        out_specs=pl.BlockSpec(memory_space=pl.ANY),
        compiler_params=pltpu.CompilerParams(vmem_limit_bytes=vmem),
        name="place_z",
    )(u)


def shifted(shard, axis, by):
    count = lax.axis_size(axis)
    return lax.ppermute(shard, axis, [(i, (i + by) % count) for i in range(count)])


def linked(shard, pairs):
    return lax.ppermute(shard, "gy", pairs)


def along_z(u):
    up, down = edges_z(u)
    high = shifted(down, "gz", -1)
    low = shifted(up, "gz", 1)
    local_z, local_y = local_parts(u)
    return join_z(local_z, low, high), local_y


def per_device(velocity):
    shape = velocity.shape
    u = velocity.reshape(shape[0] * shape[1], shape[2], shape[3])
    count, width = lax.axis_size("gy"), lax.axis_size("gz")
    row, place = lax.axis_index("gy"), lax.axis_index("gy") % column
    slow = (lax.axis_index("gz") == 0) & (row < 2)
    ends = range(count)
    final = [(i, i ^ 1) for i in ends if i % column >= column - 2]
    inner = [(i, i + 1) for i in ends if 1 <= i % column < column - 2]
    wrap = [(i, (i + 1) % count) for i in ends if i % column == column - 1]
    last = [(0, width), (width, 0)]
    first = [(i * width + k, (i ^ 1) * width + k) for i in ends if i % column < 2 for k in range(width)]
    first = [link for link in first if link not in last]

    def back(pairs):
        return [(b, a) for a, b in pairs]

    def early(u, up, down, pair):
        pair_in = lax.ppermute(pair, ("gy", "gz"), first)
        low = linked(up, inner)
        high = linked(down, back(inner))
        u, pair, pair_in = lax.optimization_barrier((u, pair, pair_in))
        u, high = lax.optimization_barrier((u, high))
        deriv_z, local_y = along_z(u)
        pair_in = jnp.where(slow, lax.ppermute(pair, ("gy", "gz"), last), pair_in)
        return deriv_z, local_y, jnp.where(place == 1, pair_in, low), jnp.where(place == 0, pair_in, high)

    def skip(u, up, down, pair):
        return place_z(u), jnp.zeros_like(u), jnp.zeros_like(up), jnp.zeros_like(down)

    u, up, down, up_in, down_in, pair = edges(u)
    low_wrap = linked(up, wrap)
    deriv_z, local_y, low, high = lax.cond(place == column - 1, skip, early, u, up_in, down_in, pair)
    down, deriv_z, local_y, low, high = lax.optimization_barrier((down, deriv_z, local_y, low, high))
    high_wrap = linked(down, back(wrap))
    deriv_z, local_y = lax.cond(place == column - 1, lambda u, z, y: along_z(u), lambda u, z, y: (z, y), u, deriv_z, local_y)
    pair, high, deriv_z, local_y = lax.optimization_barrier((pair, high, deriv_z, local_y))
    high = lax.cond(place >= column - 2, lambda pair, high: linked(pair, final), lambda pair, high: high, pair, high)
    deriv_y = join(local_y, low_wrap, low, high)
    deriv_y = join_last(deriv_y, local_y, high, high_wrap)
    return deriv_y.reshape(shape), deriv_z.reshape(shape)


def solution(mesh):
    in_specs = (P(None, None, "gy", "gz"),)
    out_specs = (P(None, None, "gy", "gz"), P(None, None, "gy", "gz"))
    return jax.shard_map(
        per_device, mesh=mesh, in_specs=in_specs, out_specs=out_specs, check_vma=False
    )
```

```python
import math

import jax
import jax.numpy as jnp
import numpy as np
from jax import lax
from jax.experimental import pallas as pl
from jax.experimental.pallas import tpu as pltpu
from jax.sharding import PartitionSpec as P

best = lax.Precision.HIGHEST
vmem = 4 << 20
column = 8
root = 1.5 - math.sqrt(5.0) / 2.0
log_root = math.log2(root)


def response(n):
    scale = root * 3.0 / (1.0 - root * root)

    def green(n):
        return scale * (-1.0) ** abs(n) * root ** abs(n)

    return 7.0 / 9.0 * (green(n + 1) - green(n - 1)) + 1.0 / 36.0 * (green(n + 2) - green(n - 2))


far_scale = response(2) / root**2
near_extra = response(1) + far_scale * root


def decay(n):
    return jnp.where(n % 2 == 0, 1.0, -1.0) * jnp.exp2(n.astype(jnp.float32) * log_root)


def operator(shape, row_start, row_dim):
    lag = row_start + lax.broadcasted_iota(jnp.int32, shape, row_dim) - lax.broadcasted_iota(jnp.int32, shape, 1 - row_dim)
    size = jnp.abs(lag)
    weight = far_scale * decay(size) + jnp.where(size == 1, near_extra, 0.0)
    return jnp.where(lag == 0, 0.0, jnp.where(lag > 0, weight, -weight))


def edges_kernel(u_hbm, u_ref, up_ref, down_ref, up_in_ref, down_in_ref, pair_ref, sem):
    planes, ny, nz = u_ref.shape
    even = lax.axis_index("gy") % 2 == 0
    copies = [pltpu.make_async_copy(u_hbm.at[p], u_ref.at[p], sem.at[p]) for p in range(planes)]
    for copy in copies:
        copy.start()
    row = lax.broadcasted_iota(jnp.int32, (ny, nz), 0)
    up_weight = far_scale * decay(ny + 1 - row)
    down_weight = -far_scale * decay(row + 2)
    for p in range(planes):
        copies[p].wait()
        u = u_ref[p]
        up = jnp.sum(u * up_weight, axis=0, keepdims=True)
        down = jnp.sum(u * down_weight, axis=0, keepdims=True)
        up_near = up * (-1.0 / root) + near_extra * u[ny - 1 : ny]
        down_near = down * (-1.0 / root) - near_extra * u[0:1]
        for ref in (up_ref, up_in_ref):
            ref[p, 0:1, :] = up_near
            ref[p, 1:2, :] = up
        for ref in (down_ref, down_in_ref):
            ref[p, 0:1, :] = down
            ref[p, 1:2, :] = down_near
        pair_ref[p, 0:1, :] = jnp.where(even, up_near, down)
        pair_ref[p, 1:2, :] = jnp.where(even, up, down_near)


def edges(u):
    planes, ny, nz = u.shape
    out = pltpu.VMEM((planes, 2, nz), jnp.float32)
    return pl.pallas_call(
        edges_kernel,
        out_shape=(pltpu.VMEM(u.shape, jnp.float32),) + (out,) * 5,
        in_specs=[pl.BlockSpec(memory_space=pl.ANY)],
        out_specs=(pl.BlockSpec(memory_space=pltpu.VMEM),) * 6,
        scratch_shapes=[pltpu.SemaphoreType.DMA((planes,))],
        compiler_params=pltpu.CompilerParams(vmem_limit_bytes=vmem),
        name="edges_y",
    )(pltpu.with_memory_space_constraint(u, pltpu.HBM))


def join_rows(local_ref, low_of, high_of, out_hbm, out_ref, sem):
    planes, ny, nz = local_ref.shape
    row = lax.broadcasted_iota(jnp.int32, (ny, nz), 0)
    low_decay = decay(jnp.maximum(row - 1, 0))
    high_decay = decay(jnp.maximum(ny - 2 - row, 0))
    copies = []
    for p in range(planes):
        low, high = low_of(p), high_of(p)
        low = jnp.where(row == 0, low[0:1], low[1:2] * low_decay)
        high = jnp.where(row == ny - 1, high[1:2], high[0:1] * high_decay)
        out_ref[p] = local_ref[p] + low + high
        copies.append(pltpu.make_async_copy(out_ref.at[p], out_hbm.at[p], sem.at[p]))
        copies[p].start()
    for copy in copies:
        copy.wait()


def join_kernel(local_ref, wrap_ref, low_ref, high_ref, out_hbm, out_ref, sem):
    place = lax.axis_index("gy") % column

    @pl.when(place != column - 1)
    def _():
        def low(p):
            return jnp.where(place == 0, wrap_ref[p], low_ref[p])

        join_rows(local_ref, low, lambda p: high_ref[p], out_hbm, out_ref, sem)


def join_last_kernel(made_hbm, local_ref, low_ref, wrap_ref, out_hbm, out_ref, sem):
    @pl.when(lax.axis_index("gy") % column == column - 1)
    def _():
        join_rows(local_ref, lambda p: low_ref[p], lambda p: wrap_ref[p], out_hbm, out_ref, sem)


def join(local, *ends):
    planes = local.shape[0]
    return pl.pallas_call(
        join_kernel,
        out_shape=jax.ShapeDtypeStruct(local.shape, jnp.float32),
        in_specs=[pl.BlockSpec(memory_space=pltpu.VMEM)] * 4,
        out_specs=pl.BlockSpec(memory_space=pl.ANY),
        scratch_shapes=[pltpu.VMEM(local.shape, jnp.float32), pltpu.SemaphoreType.DMA((planes,))],
        compiler_params=pltpu.CompilerParams(vmem_limit_bytes=vmem),
        cost_estimate=pl.CostEstimate(flops=6 * local.size, bytes_accessed=8 * local.size, transcendentals=32768),
        name="join_y",
    )(*(pltpu.with_memory_space_constraint(end, pltpu.VMEM) for end in (local, *ends)))


def join_last(made, local, low, wrap):
    planes = local.shape[0]
    return pl.pallas_call(
        join_last_kernel,
        out_shape=jax.ShapeDtypeStruct(local.shape, jnp.float32),
        in_specs=[pl.BlockSpec(memory_space=pl.ANY)] + [pl.BlockSpec(memory_space=pltpu.VMEM)] * 3,
        out_specs=pl.BlockSpec(memory_space=pl.ANY),
        scratch_shapes=[pltpu.VMEM(local.shape, jnp.float32), pltpu.SemaphoreType.DMA((planes,))],
        compiler_params=pltpu.CompilerParams(vmem_limit_bytes=vmem),
        input_output_aliases={0: 0},
        name="join_y_last",
    )(made, *(pltpu.with_memory_space_constraint(end, pltpu.VMEM) for end in (local, low, wrap)))


def edges_z_kernel(u_ref, up_ref, down_ref):
    planes, ny, nz = u_ref.shape
    which = lax.broadcasted_iota(jnp.int32, (8, nz), 0)
    cell = lax.broadcasted_iota(jnp.int32, (8, nz), 1)
    target = jnp.where(which < 2, nz + which, which - 4)
    lag = target - cell
    size = jnp.abs(lag)
    weight = far_scale * decay(size) + jnp.where(size == 1, near_extra, 0.0)
    weight = jnp.where(lag > 0, weight, -weight)
    ends = lax.dot_general(
        weight, u_ref[...].reshape(planes * ny, nz), (((1,), (1,)), ((), ())), precision=best, preferred_element_type=jnp.float32
    )
    up_ref[...] = ends[0:2]
    down_ref[...] = ends[2:4]


def edges_z(u):
    out = jax.ShapeDtypeStruct((2, u.shape[0] * u.shape[1]), jnp.float32)
    here = pl.BlockSpec(memory_space=pltpu.VMEM)
    return pl.pallas_call(
        edges_z_kernel,
        out_shape=(out, out),
        in_specs=[here],
        out_specs=(here, here),
        compiler_params=pltpu.CompilerParams(vmem_limit_bytes=vmem),
        name="edges_z",
    )(u)


def local_kernel(u_ref, z_ref, y_ref):
    planes, ny, nz = u_ref.shape
    lines = u_ref[...].reshape(planes * ny, nz)
    across = operator((ny, ny), 0, 0)
    along_z = jnp.dot(lines, operator((nz, nz), 0, 1), precision=best, preferred_element_type=jnp.float32)
    z_ref[...] = along_z.reshape(planes, ny, nz)
    for p in range(planes):
        y_ref[p] = jnp.dot(across, u_ref[p], precision=best, preferred_element_type=jnp.float32)


def local_parts(u, flops):
    out = jax.ShapeDtypeStruct(u.shape, jnp.float32)
    here = pl.BlockSpec(memory_space=pltpu.VMEM)
    return pl.pallas_call(
        local_kernel,
        out_shape=(out, out),
        in_specs=[here],
        out_specs=(here, here),
        compiler_params=pltpu.CompilerParams(vmem_limit_bytes=vmem),
        cost_estimate=pl.CostEstimate(flops=flops, bytes_accessed=12 * u.size, transcendentals=70000),
        name="local_parts",
    )(u)


def join_z_kernel(local_ref, high_ref, low_ref, out_ref):
    planes, ny, nz = local_ref.shape
    ends = jnp.concatenate([low_ref[...], high_ref[...], low_ref[...], high_ref[...]], axis=0)
    ends = jnp.transpose(ends)
    cell = lax.broadcasted_iota(jnp.int32, (1, nz), 1)
    low_first = jnp.where(cell == 0, 1.0, 0.0)
    low_rest = jnp.where(cell == 0, 0.0, decay(jnp.maximum(cell - 1, 0)))
    high_first = jnp.where(cell == nz - 1, 1.0, 0.0)
    high_rest = jnp.where(cell == nz - 1, 0.0, decay(jnp.maximum(nz - 2 - cell, 0)))
    for p in range(planes):
        end = ends[p * ny : (p + 1) * ny]
        low = end[:, 0:1] * low_first + end[:, 1:2] * low_rest
        high = end[:, 2:3] * high_rest + end[:, 3:4] * high_first
        out_ref[p] = local_ref[p] + low + high


def join_z(local, low, high):
    here = pl.BlockSpec(memory_space=pltpu.VMEM)
    return pl.pallas_call(
        join_z_kernel,
        out_shape=jax.ShapeDtypeStruct(local.shape, jnp.float32),
        in_specs=[here] * 3,
        out_specs=here,
        compiler_params=pltpu.CompilerParams(vmem_limit_bytes=vmem),
        name="join_z",
    )(local, high, low)


def place_kernel(u_hbm, out_hbm):
    pass


def place_z(u):
    return pl.pallas_call(
        place_kernel,
        out_shape=jax.ShapeDtypeStruct(u.shape, u.dtype),
        in_specs=[pl.BlockSpec(memory_space=pl.ANY)],
        out_specs=pl.BlockSpec(memory_space=pl.ANY),
        compiler_params=pltpu.CompilerParams(vmem_limit_bytes=vmem),
        name="place_z",
    )(u)


def shifted(shard, axis, by):
    count = lax.axis_size(axis)
    return lax.ppermute(shard, axis, [(i, (i + by) % count) for i in range(count)])


def linked(shard, pairs):
    return lax.ppermute(shard, "gy", pairs)


def along_z(u, flops):
    up, down = edges_z(u)
    high = shifted(down, "gz", -1)
    low = shifted(up, "gz", 1)
    local_z, local_y = local_parts(u, flops)
    return join_z(local_z, low, high), local_y


def per_device(velocity):
    shape = velocity.shape
    u = velocity.reshape(shape[0] * shape[1], shape[2], shape[3])
    count, width = lax.axis_size("gy"), lax.axis_size("gz")
    row, place = lax.axis_index("gy"), lax.axis_index("gy") % column
    slow = (lax.axis_index("gz") == 0) & (row < 2)
    ends = range(count)
    final = [(i, i ^ 1) for i in ends if i % column >= column - 2]
    inner = [(i, i + 1) for i in ends if 1 <= i % column < column - 2]
    wrap = [(i, (i + 1) % count) for i in ends if i % column == column - 1]
    last = [(0, width), (width, 0)]
    first = [(i * width + k, (i ^ 1) * width + k) for i in ends if i % column < 2 for k in range(width)]
    first = [link for link in first if link not in last]

    def back(pairs):
        return [(b, a) for a, b in pairs]

    def early(u, up, down, pair):
        pair_in = lax.ppermute(pair, ("gy", "gz"), first)
        low = linked(up, inner)
        high = linked(down, back(inner))
        u, pair, pair_in = lax.optimization_barrier((u, pair, pair_in))
        u, high = lax.optimization_barrier((u, high))
        deriv_z, local_y = along_z(u, 10**9)
        pair_in = jnp.where(slow, lax.ppermute(pair, ("gy", "gz"), last), pair_in)
        return deriv_z, local_y, jnp.where(place == 1, pair_in, low), jnp.where(place == 0, pair_in, high)

    def skip(u, up, down, pair):
        return place_z(u), jnp.zeros_like(u), jnp.zeros_like(up), jnp.zeros_like(down)

    u, up, down, up_in, down_in, pair = edges(u)
    low_wrap = linked(up, wrap)
    deriv_z, local_y, low, high = lax.cond(place == column - 1, skip, early, u, up_in, down_in, pair)
    down, deriv_z, local_y, low, high = lax.optimization_barrier((down, deriv_z, local_y, low, high))
    high_wrap = linked(down, back(wrap))
    deriv_z, local_y = lax.cond(place == column - 1, lambda u, z, y: along_z(u, 10**8), lambda u, z, y: (z, y), u, deriv_z, local_y)
    pair, high, deriv_z, local_y = lax.optimization_barrier((pair, high, deriv_z, local_y))
    high = lax.cond(place >= column - 2, lambda pair, high: linked(pair, final), lambda pair, high: high, pair, high)
    deriv_y = join(local_y, low_wrap, low, high)
    deriv_y = join_last(deriv_y, local_y, high, high_wrap)
    return deriv_y.reshape(shape), deriv_z.reshape(shape)


def solution(mesh):
    in_specs = (P(None, None, "gy", "gz"),)
    out_specs = (P(None, None, "gy", "gz"), P(None, None, "gy", "gz"))
    return jax.shard_map(
        per_device, mesh=mesh, in_specs=in_specs, out_specs=out_specs, check_vma=False
    )
```

```python
import math

import jax
import jax.numpy as jnp
import numpy as np
from jax import lax
from jax.experimental import pallas as pl
from jax.experimental.pallas import tpu as pltpu
from jax.sharding import PartitionSpec as P

best = lax.Precision.HIGHEST
vmem = 4 << 20
column = 8
root = 1.5 - math.sqrt(5.0) / 2.0
log_root = math.log2(root)


def response(n):
    scale = root * 3.0 / (1.0 - root * root)

    def green(n):
        return scale * (-1.0) ** abs(n) * root ** abs(n)

    return 7.0 / 9.0 * (green(n + 1) - green(n - 1)) + 1.0 / 36.0 * (green(n + 2) - green(n - 2))


far_scale = response(2) / root**2
near_extra = response(1) + far_scale * root


def decay(n):
    return jnp.where(n % 2 == 0, 1.0, -1.0) * jnp.exp2(n.astype(jnp.float32) * log_root)


def operator(shape, row_start, row_dim):
    lag = row_start + lax.broadcasted_iota(jnp.int32, shape, row_dim) - lax.broadcasted_iota(jnp.int32, shape, 1 - row_dim)
    size = jnp.abs(lag)
    weight = far_scale * decay(size) + jnp.where(size == 1, near_extra, 0.0)
    return jnp.where(lag == 0, 0.0, jnp.where(lag > 0, weight, -weight))


def edges_kernel(u_hbm, u_ref, up_ref, down_ref, up_in_ref, down_in_ref, pair_ref, sem):
    planes, ny, nz = u_ref.shape
    even = lax.axis_index("gy") % 2 == 0
    copies = [pltpu.make_async_copy(u_hbm.at[p], u_ref.at[p], sem.at[p]) for p in range(planes)]
    for copy in copies:
        copy.start()
    row = lax.broadcasted_iota(jnp.int32, (ny, nz), 0)
    up_weight = far_scale * decay(ny + 1 - row)
    down_weight = -far_scale * decay(row + 2)
    for p in range(planes):
        copies[p].wait()
        u = u_ref[p]
        up = jnp.sum(u * up_weight, axis=0, keepdims=True)
        down = jnp.sum(u * down_weight, axis=0, keepdims=True)
        up_near = up * (-1.0 / root) + near_extra * u[ny - 1 : ny]
        down_near = down * (-1.0 / root) - near_extra * u[0:1]
        for ref in (up_ref, up_in_ref):
            ref[p, 0:1, :] = up_near
            ref[p, 1:2, :] = up
        for ref in (down_ref, down_in_ref):
            ref[p, 0:1, :] = down
            ref[p, 1:2, :] = down_near
        pair_ref[p, 0:1, :] = jnp.where(even, up_near, down)
        pair_ref[p, 1:2, :] = jnp.where(even, up, down_near)


def edges(u):
    planes, ny, nz = u.shape
    out = pltpu.VMEM((planes, 2, nz), jnp.float32)
    return pl.pallas_call(
        edges_kernel,
        out_shape=(pltpu.VMEM(u.shape, jnp.float32),) + (out,) * 5,
        in_specs=[pl.BlockSpec(memory_space=pl.ANY)],
        out_specs=(pl.BlockSpec(memory_space=pltpu.VMEM),) * 6,
        scratch_shapes=[pltpu.SemaphoreType.DMA((planes,))],
        compiler_params=pltpu.CompilerParams(vmem_limit_bytes=vmem),
        name="edges_y",
    )(pltpu.with_memory_space_constraint(u, pltpu.HBM))


def join_rows(local_ref, low_of, high_of, out_hbm, out_ref, sem):
    planes, ny, nz = local_ref.shape
    row = lax.broadcasted_iota(jnp.int32, (ny, nz), 0)
    low_decay = decay(jnp.maximum(row - 1, 0))
    high_decay = decay(jnp.maximum(ny - 2 - row, 0))
    copies = []
    for p in range(planes):
        low, high = low_of(p), high_of(p)
        low = jnp.where(row == 0, low[0:1], low[1:2] * low_decay)
        high = jnp.where(row == ny - 1, high[1:2], high[0:1] * high_decay)
        out_ref[p] = local_ref[p] + low + high
        copies.append(pltpu.make_async_copy(out_ref.at[p], out_hbm.at[p], sem.at[p]))
        copies[p].start()
    for copy in copies:
        copy.wait()


def join_kernel(local_ref, wrap_ref, low_ref, high_ref, out_hbm, out_ref, sem):
    place = lax.axis_index("gy") % column

    @pl.when(place != column - 1)
    def _():
        def low(p):
            return jnp.where(place == 0, wrap_ref[p], low_ref[p])

        join_rows(local_ref, low, lambda p: high_ref[p], out_hbm, out_ref, sem)


def join_last_kernel(made_hbm, local_ref, low_ref, wrap_ref, out_hbm, out_ref, sem):
    @pl.when(lax.axis_index("gy") % column == column - 1)
    def _():
        join_rows(local_ref, lambda p: low_ref[p], lambda p: wrap_ref[p], out_hbm, out_ref, sem)


def join(local, *ends):
    planes = local.shape[0]
    return pl.pallas_call(
        join_kernel,
        out_shape=jax.ShapeDtypeStruct(local.shape, jnp.float32),
        in_specs=[pl.BlockSpec(memory_space=pltpu.VMEM)] * 4,
        out_specs=pl.BlockSpec(memory_space=pl.ANY),
        scratch_shapes=[pltpu.VMEM(local.shape, jnp.float32), pltpu.SemaphoreType.DMA((planes,))],
        compiler_params=pltpu.CompilerParams(vmem_limit_bytes=vmem),
        cost_estimate=pl.CostEstimate(flops=6 * local.size, bytes_accessed=8 * local.size, transcendentals=32768),
        name="join_y",
    )(*(pltpu.with_memory_space_constraint(end, pltpu.VMEM) for end in (local, *ends)))


def join_last(made, local, low, wrap):
    planes = local.shape[0]
    return pl.pallas_call(
        join_last_kernel,
        out_shape=jax.ShapeDtypeStruct(local.shape, jnp.float32),
        in_specs=[pl.BlockSpec(memory_space=pl.ANY)] + [pl.BlockSpec(memory_space=pltpu.VMEM)] * 3,
        out_specs=pl.BlockSpec(memory_space=pl.ANY),
        scratch_shapes=[pltpu.VMEM(local.shape, jnp.float32), pltpu.SemaphoreType.DMA((planes,))],
        compiler_params=pltpu.CompilerParams(vmem_limit_bytes=vmem),
        input_output_aliases={0: 0},
        name="join_y_last",
    )(made, *(pltpu.with_memory_space_constraint(end, pltpu.VMEM) for end in (local, low, wrap)))


def edges_z_kernel(u_ref, up_ref, down_ref):
    planes, ny, nz = u_ref.shape
    which = lax.broadcasted_iota(jnp.int32, (8, nz), 0)
    cell = lax.broadcasted_iota(jnp.int32, (8, nz), 1)
    target = jnp.where(which < 2, nz + which, which - 4)
    lag = target - cell
    size = jnp.abs(lag)
    weight = far_scale * decay(size) + jnp.where(size == 1, near_extra, 0.0)
    weight = jnp.where(lag > 0, weight, -weight)
    ends = lax.dot_general(
        weight, u_ref[...].reshape(planes * ny, nz), (((1,), (1,)), ((), ())), precision=best, preferred_element_type=jnp.float32
    )
    up_ref[...] = ends[0:2]
    down_ref[...] = ends[2:4]


def edges_z(u):
    out = jax.ShapeDtypeStruct((2, u.shape[0] * u.shape[1]), jnp.float32)
    here = pl.BlockSpec(memory_space=pltpu.VMEM)
    return pl.pallas_call(
        edges_z_kernel,
        out_shape=(out, out),
        in_specs=[here],
        out_specs=(here, here),
        compiler_params=pltpu.CompilerParams(vmem_limit_bytes=vmem),
        name="edges_z",
    )(u)


def local_kernel(u_ref, z_ref, y_ref):
    planes, ny, nz = u_ref.shape
    lines = u_ref[...].reshape(planes * ny, nz)
    across = operator((ny, ny), 0, 0)
    along_z = jnp.dot(lines, operator((nz, nz), 0, 1), precision=best, preferred_element_type=jnp.float32)
    z_ref[...] = along_z.reshape(planes, ny, nz)
    for p in range(planes):
        y_ref[p] = jnp.dot(across, u_ref[p], precision=best, preferred_element_type=jnp.float32)


def local_parts(u, flops):
    out = jax.ShapeDtypeStruct(u.shape, jnp.float32)
    here = pl.BlockSpec(memory_space=pltpu.VMEM)
    return pl.pallas_call(
        local_kernel,
        out_shape=(out, out),
        in_specs=[here],
        out_specs=(here, here),
        compiler_params=pltpu.CompilerParams(vmem_limit_bytes=vmem),
        cost_estimate=pl.CostEstimate(flops=flops, bytes_accessed=12 * u.size, transcendentals=70000),
        name="local_parts",
    )(u)


def join_z_kernel(local_ref, high_ref, low_ref, out_hbm, out_ref, sem):
    planes, ny, nz = local_ref.shape
    ends = jnp.concatenate([low_ref[...], high_ref[...], low_ref[...], high_ref[...]], axis=0)
    ends = jnp.transpose(ends)
    cell = lax.broadcasted_iota(jnp.int32, (1, nz), 1)
    low_first = jnp.where(cell == 0, 1.0, 0.0)
    low_rest = jnp.where(cell == 0, 0.0, decay(jnp.maximum(cell - 1, 0)))
    high_first = jnp.where(cell == nz - 1, 1.0, 0.0)
    high_rest = jnp.where(cell == nz - 1, 0.0, decay(jnp.maximum(nz - 2 - cell, 0)))
    for p in range(planes):
        end = ends[p * ny : (p + 1) * ny]
        low = end[:, 0:1] * low_first + end[:, 1:2] * low_rest
        high = end[:, 2:3] * high_rest + end[:, 3:4] * high_first
        out_ref[p] = local_ref[p] + low + high
    copy = pltpu.make_async_copy(out_ref, out_hbm, sem)
    copy.start()
    copy.wait()


def join_z(local, low, high):
    here = pl.BlockSpec(memory_space=pltpu.VMEM)
    return pl.pallas_call(
        join_z_kernel,
        out_shape=pltpu.HBM(local.shape, jnp.float32),
        in_specs=[here] * 3,
        out_specs=pl.BlockSpec(memory_space=pl.ANY),
        scratch_shapes=[pltpu.VMEM(local.shape, jnp.float32), pltpu.SemaphoreType.DMA],
        compiler_params=pltpu.CompilerParams(vmem_limit_bytes=vmem),
        name="join_z",
    )(local, high, low)


def place_kernel(u_hbm, out_hbm):
    pass


def place_z(u):
    return pl.pallas_call(
        place_kernel,
        out_shape=pltpu.HBM(u.shape, u.dtype),
        in_specs=[pl.BlockSpec(memory_space=pl.ANY)],
        out_specs=pl.BlockSpec(memory_space=pl.ANY),
        compiler_params=pltpu.CompilerParams(vmem_limit_bytes=vmem),
        name="place_z",
    )(u)


def shifted(shard, axis, by):
    count = lax.axis_size(axis)
    return lax.ppermute(shard, axis, [(i, (i + by) % count) for i in range(count)])


def linked(shard, pairs):
    return lax.ppermute(shard, "gy", pairs)


def along_z(u, flops):
    up, down = edges_z(u)
    high = shifted(down, "gz", -1)
    low = shifted(up, "gz", 1)
    local_z, local_y = local_parts(u, flops)
    return join_z(local_z, low, high), local_y


def per_device(velocity):
    shape = velocity.shape
    u = velocity.reshape(shape[0] * shape[1], shape[2], shape[3])
    count, width = lax.axis_size("gy"), lax.axis_size("gz")
    row, place = lax.axis_index("gy"), lax.axis_index("gy") % column
    slow = (lax.axis_index("gz") == 0) & (row < 2)
    ends = range(count)
    final = [(i, i ^ 1) for i in ends if i % column >= column - 2]
    inner = [(i, i + 1) for i in ends if 1 <= i % column < column - 2]
    wrap = [(i, (i + 1) % count) for i in ends if i % column == column - 1]
    last = [(0, width), (width, 0)]
    first = [(i * width + k, (i ^ 1) * width + k) for i in ends if i % column < 2 for k in range(width)]
    first = [link for link in first if link not in last]

    def back(pairs):
        return [(b, a) for a, b in pairs]

    def early(u, up, down, pair):
        pair_in = lax.ppermute(pair, ("gy", "gz"), first)
        low = linked(up, inner)
        high = linked(down, back(inner))
        u, pair, pair_in = lax.optimization_barrier((u, pair, pair_in))
        u, high = lax.optimization_barrier((u, high))
        deriv_z, local_y = along_z(u, 10**9)
        pair_in = jnp.where(slow, lax.ppermute(pair, ("gy", "gz"), last), pair_in)
        return deriv_z, local_y, jnp.where(place == 1, pair_in, low), jnp.where(place == 0, pair_in, high)

    def skip(u, up, down, pair):
        return place_z(u), jnp.zeros_like(u), jnp.zeros_like(up), jnp.zeros_like(down)

    u, up, down, up_in, down_in, pair = edges(u)
    low_wrap = linked(up, wrap)
    deriv_z, local_y, low, high = lax.cond(place == column - 1, skip, early, u, up_in, down_in, pair)
    down, deriv_z, local_y, low, high = lax.optimization_barrier((down, deriv_z, local_y, low, high))
    high_wrap = linked(down, back(wrap))
    deriv_z, local_y = lax.cond(place == column - 1, lambda u, z, y: along_z(u, 10**8), lambda u, z, y: (z, y), u, deriv_z, local_y)
    pair, high, deriv_z, local_y = lax.optimization_barrier((pair, high, deriv_z, local_y))
    high = lax.cond(place >= column - 2, lambda pair, high: linked(pair, final), lambda pair, high: high, pair, high)
    deriv_y = join(local_y, low_wrap, low, high)
    deriv_y = join_last(deriv_y, local_y, high, high_wrap)
    return deriv_y.reshape(shape), deriv_z.reshape(shape)


def solution(mesh):
    in_specs = (P(None, None, "gy", "gz"),)
    out_specs = (P(None, None, "gy", "gz"), P(None, None, "gy", "gz"))
    return jax.shard_map(
        per_device, mesh=mesh, in_specs=in_specs, out_specs=out_specs, check_vma=False
    )
```
